32 devices in a mesh: groups: 2 (over x), ha: 2 (over core), wa: 8 (over z, y).
Axes of the slice: x: 2, y: 2, z: 4, core: 2. Of those that a mesh axis runs over, the one named last changes fastest.
Arguments:
- queries: bfloat16 [16, 16, 64, 1536], P('groups', 'ha', 'wa'), parts along dimension 0, may hold values from -40 to 40
- keys: bfloat16 [16, 16, 64, 1536], P('groups', 'ha', 'wa'), parts along dimension 0, may hold values from -40 to 40
- values: bfloat16 [16, 16, 64, 1536], P('groups', 'ha', 'wa'), parts along dimension 0, may hold values from -6 to 6
- tile_map: int32 [2, 8, 8], P('ha', 'wa'), may hold values 0 or 1
- frame_offset: int32 [2, 8], P('ha', 'wa'), may hold values from -2 to 2
- out_weight: bfloat16 [1536, 3072], P(None, ('ha', 'wa')), may hold values from -0.15625 to 0.15625
- out_bias: float32 [3072], replicated, may hold values from -1 to 1
- out_gate: float32 [6144], P('groups'), parts along dimension 0, may hold values from 0.5 to 2
Outputs:
- branch: bfloat16 [16, 16, 64, 3072], P('groups', 'ha', 'wa'), parts along dimension 0
The draws below stay inside these ranges and needn't reach their ends.
There are 2 independent parts, one for each index of `groups`. The reference program is written for one: setup_inputs(seed, part) draws one part's arguments, and reference() takes and returns one part's arrays. A program takes and returns all parts, laid end to end along the dimension named above; an argument that names none is the same for every part. Nothing has to cross between parts.
All inputs are finite; a program needn't handle non-finite values. No bound on the sum of `tile_map` on one device may be relied on, other than what follows from the above.
Results may differ from the reference program's by a relative error of at most 0.01.
Values may be sent and summed in bfloat16 or wider, within the bound.
No kernel may reach another device: no remote copies, remote signals or barrier semaphores. Data moves between devices by JAX's collectives and lax.ppermute only.
A program may use at most 192 MiB of HBM per device.

```python
import jax
import jax.numpy as jnp
from jax import lax

D = 3072
HEADS = 12
HEAD_DIM = 128
F = 8
TH = 8
TW = 8
RADIUS = 2
H = 16
W = 64
HC = 1536
N_HA = 2
N_WA = 8


def paired_fields(key):
    shape = (F, H, W, HEADS * HEAD_DIM)
    key_q = jax.random.fold_in(key, 11)
    key_k = jax.random.fold_in(key, 12)
    query_field = 1.5 * jax.random.truncated_normal(key_q, -4.0, 4.0, shape, jnp.float32)
    key_field = 1.5 * jax.random.truncated_normal(key_k, -4.0, 4.0, shape, jnp.float32)
    return (jnp.clip(query_field, -40.0, 40.0), jnp.clip(key_field, -40.0, 40.0))


def draw_queries(key, part):
    return paired_fields(key)[0].astype(jnp.bfloat16)


def draw_keys(key, part):
    return paired_fields(key)[1].astype(jnp.bfloat16)


def with_ends(drawn, rng, low, high):
    dims = drawn.shape
    spot = [jax.random.randint(jax.random.fold_in(rng, axis), (), 0, dims[axis]) for axis in range(len(dims))]
    drawn = drawn.at[tuple(spot)].set(low)
    longest = dims.index(max(dims))
    spot[longest] = (spot[longest] + 1) % dims[longest]
    return drawn.at[tuple(spot)].set(high)


def block_levels(key, extent, shards, least, top_value):
    gain, own = 1.0, jax.random.fold_in(key, 6)
    for position, shards_of in shards:
        heights = jnp.exp(jax.random.uniform(jax.random.fold_in(own, position), (shards_of,), jnp.float32, least / len(shards), top_value / len(shards)))
        gain = gain * jnp.repeat(heights, extent[position] // shards_of).reshape([-1 if axis == position else 1 for axis in range(len(extent))])
    return gain


def gaussian(own_key, shape, scale, bound, cuts=(), held_as=jnp.bfloat16):
    result = jax.random.normal(own_key, shape, jnp.float32) * scale
    if len(cuts) > 0:
        result = block_levels(own_key, shape, cuts, -0.22, 0.18) * result
    return jnp.clip(result, min=-bound, max=bound).astype(held_as)


def setup_inputs(seed: int = 0, part: int = 0) -> dict:
    arg_keys = jax.random.split(jax.random.key(seed), 9)
    own_keys = jax.random.split(jax.random.fold_in(arg_keys[8], part), 9)
    queries = draw_queries(jax.random.fold_in(jax.random.fold_in(arg_keys[8], part), 71), part)
    keys = draw_keys(jax.random.fold_in(jax.random.fold_in(arg_keys[8], part), 71), part)
    values = gaussian(own_keys[2], (F, H, W, HC), 1.0, 6.0, ((1, 2), (2, 8)))
    tile_map = with_ends((jax.random.randint(arg_keys[3], (N_HA, N_WA, 8), 0, 4) < 3).astype(jnp.int32), jax.random.fold_in(arg_keys[3], 1), 0, 1)
    frame_offset = with_ends(jax.random.randint(arg_keys[4], (N_HA, N_WA), -2, 3), jax.random.fold_in(arg_keys[4], 1), -2, 2).astype(jnp.int32)
    out_weight = gaussian(arg_keys[5], (HC, D), HC ** -0.5, 0.15625, ((1, 16),))
    out_bias = gaussian(arg_keys[6], (D,), 0.2, 1.0, (), jnp.float32)
    out_gate = jnp.clip(jax.random.uniform(own_keys[7], (D,), jnp.float32, 0.5, 2.0), 0.5, 2.0)
    return dict(queries=queries, keys=keys, values=values, tile_map=tile_map, frame_offset=frame_offset, out_weight=out_weight, out_bias=out_bias, out_gate=out_gate)


def beside_all(index, count):
    spots = jnp.arange(3, dtype=jnp.int32) - 1
    return (index + spots >= 0) & (index + spots < count)


def tile_flags(row_map, inside_h, inside_w):
    full = jnp.concatenate([row_map[:4], jnp.ones((1,), jnp.int32), row_map[4:]]) > 0
    return full & (inside_h[:, None] & inside_w[None, :]).reshape(9)


def key_mask(flags, offset, frames, tile_h, tile_w):
    frame_ids = jnp.arange(frames, dtype=jnp.int32)
    time_ok = jnp.abs(frame_ids[None, :] - frame_ids[:, None] - offset) <= RADIUS
    rows = jnp.arange(3 * tile_h, dtype=jnp.int32) // tile_h
    cols = jnp.arange(3 * tile_w, dtype=jnp.int32) // tile_w
    tile_of = rows[:, None] * 3 + cols[None, :]
    hits = (tile_of[:, :, None] == jnp.arange(9, dtype=jnp.int32)[None, None, :]) & flags[None, None, :]
    tile_on = jnp.any(hits, axis=2)
    centre = tile_of == 4
    allowed = centre[None, None] | (tile_on[None, None] & time_ok[:, :, None, None])
    return allowed.reshape(frames, -1)


def reference(queries, keys, values, tile_map, frame_offset, out_weight, out_bias, out_gate):
    count_h = H // TH
    count_w = W // TW
    scale = HEAD_DIM ** -0.5
    widths = ((0, 0), (TH, TH), (TW, TW), (0, 0))
    keys_pad = jnp.pad(keys, widths)
    values_pad = jnp.pad(values, widths)

    def one_tile(index):
        row = index // count_w
        col = index % count_w
        zero = jnp.zeros((), jnp.int32)
        q_tile = lax.dynamic_slice(queries, (zero, row * TH, col * TW, zero), (F, TH, TW, HC))
        k_tile = lax.dynamic_slice(keys_pad, (zero, row * TH, col * TW, zero), (F, 3 * TH, 3 * TW, HC))
        v_tile = lax.dynamic_slice(values_pad, (zero, row * TH, col * TW, zero), (F, 3 * TH, 3 * TW, HC))
        flags = tile_flags(tile_map[row, col], beside_all(row, count_h), beside_all(col, count_w))
        allowed = key_mask(flags, frame_offset[row, col], F, TH, TW)
        q_heads = q_tile.astype(jnp.float32).reshape(F, TH * TW, HEADS, HEAD_DIM)
        k_heads = k_tile.astype(jnp.float32).reshape(-1, HEADS, HEAD_DIM)
        v_heads = v_tile.astype(jnp.float32).reshape(-1, HEADS, HEAD_DIM)
        scores = jnp.einsum('fqhd,khd->hfqk', q_heads, k_heads) * scale
        scores = jnp.where(allowed[None, :, None, :], scores, -1e30)
        top = jnp.max(scores, axis=-1, keepdims=True)
        expo = jnp.exp(scores - top)
        probs = (expo / jnp.sum(expo, axis=-1, keepdims=True)).astype(jnp.bfloat16)
        attn = jnp.einsum('hfqk,khd->fqhd', probs.astype(jnp.float32), v_heads)
        return attn.astype(jnp.bfloat16).reshape(F, TH, TW, HC)

    tiles = lax.map(one_tile, jnp.arange(count_h * count_w, dtype=jnp.int32))
    attn = tiles.reshape(count_h, count_w, F, TH, TW, HC).transpose(2, 0, 3, 1, 4, 5).reshape(F * H * W, HC)
    proj = jnp.dot(attn, out_weight, preferred_element_type=jnp.float32)
    branch = ((proj + out_bias) * out_gate).astype(jnp.bfloat16)
    return branch.reshape(F, H, W, D)
```

```python
import functools

import jax
import jax.numpy as jnp
from jax import lax
from jax.experimental import pallas as pl
from jax.experimental.pallas import tpu as pltpu
from jax.sharding import PartitionSpec as P

HEAD_DIM = 128
RADIUS = 2
LOG2E = 1.4426950408889634
NEG = -1e30
ROWS = 2


def swaps(count):
    return [(i, i ^ 1) for i in range(count)]


def outward(count):
    return [(i, i - 2) for i in range(2, count, 2)] + [(i, i + 2) for i in range(1, count - 2, 2)]


def inward(count):
    return [(i, i + 2) for i in range(0, count - 2, 2)] + [(i, i - 2) for i in range(3, count, 2)]


def flag_table(meta, a, w, count):
    side = 1 - 2 * (w % 2)
    partner = w + side
    row = jnp.stack([a, 1 - a])
    q_col = jnp.stack([partner, partner, w, w])
    q_row = jnp.concatenate([row, row])
    k_col = jnp.stack([partner, w])
    ends = jnp.stack([partner + side, w - side])
    k_cols = jnp.concatenate(
        [
            jnp.broadcast_to(jnp.repeat(k_col, 2), (4, 4)),
            jnp.repeat(jnp.repeat(ends, 2)[:, None], 2, axis=1),
        ],
        axis=1,
    )
    k_rows = jnp.broadcast_to(jnp.tile(row, 3), (4, 6))
    d_row = k_rows - q_row[:, None]
    d_col = k_cols - q_col[:, None]
    spot = (d_row + 1) * 3 + d_col + 1
    own = spot == 4
    slot = spot - (spot > 4)
    hit = slot[:, :, None] == jnp.arange(8, dtype=jnp.int32)
    chosen = jnp.sum(jnp.where(hit, meta[:, None, :8], 0), axis=2) > 0
    inside = (k_cols >= 0) & (k_cols < count)
    flags = jnp.where(own, 2, (chosen & inside).astype(jnp.int32))
    return jnp.concatenate([flags, meta[:, 8:10]], axis=1).astype(jnp.int32)


def attend_kernel(frames, block, first, index_ref, table_ref, q_refs, k_refs, v_refs, o_ref):
    row = pl.program_id(0)
    tokens = o_ref.shape[0]
    area = tokens // frames
    scale = HEAD_DIM ** (-0.5) * LOG2E
    offset = table_ref[first + row, 6]
    q_frame = lax.broadcasted_iota(jnp.int32, (frames, tokens), 0)
    k_frame = lax.broadcasted_iota(jnp.int32, (frames, tokens), 1) // area
    near = jnp.where(jnp.abs(k_frame - q_frame - offset) <= RADIUS, 1, 0)
    bias = []
    for t in range(6):
        flag = table_ref[first + row, t]
        bias.append(jnp.where((near * (flag & 1) + (flag >> 1)) > 0, 0.0, NEG).astype(jnp.float32))
    per = block // area
    for start in range(0, tokens, block):
        q = q_refs(row, start, block)
        scores = []
        for t in range(6):
            s = lax.dot_general(
                q, k_refs[t][...], (((1,), (1,)), ((), ())), preferred_element_type=jnp.float32
            )
            at = start // area
            part = bias[t][at : at + per]
            scores.append((s.reshape(per, area, tokens) + part[:, None, :]).reshape(block, tokens))
        top = functools.reduce(jnp.maximum, scores)
        top = jnp.max(top, axis=-1, keepdims=True)
        total = None
        out = None
        for t in range(6):
            p = jnp.exp2((scores[t] - top) * scale)
            total = p if total is None else total + p
            d = jnp.dot(p.astype(jnp.bfloat16), v_refs[t][...], preferred_element_type=jnp.float32)
            out = d if out is None else out + d
        total = jnp.sum(total, axis=-1, keepdims=True)
        o_ref[pl.ds(start, block), :] = (out / total).astype(o_ref.dtype)


def partner_kernel(frames, block, index_ref, table_ref, qp, kvp, k, v, kvc, end, o_ref):
    ks = [kvp.at[0, 0], kvp.at[0, 1], k, kvc.at[0], end.at[0, 0], end.at[0, 1]]
    vs = [kvp.at[1, 0], kvp.at[1, 1], v, kvc.at[1], end.at[1, 0], end.at[1, 1]]

    def q_of(row, start, size):
        return qp[pl.ds(start, size), :]

    attend_kernel(frames, block, 0, index_ref, table_ref, q_of, ks, vs, o_ref)


def own_kernel(frames, block, index_ref, table_ref, q, qc, kvp, k, v, kvc, end, o_ref):
    ks = [kvp.at[0, 0], kvp.at[0, 1], k, kvc.at[0], end.at[0, 0], end.at[0, 1]]
    vs = [kvp.at[1, 0], kvp.at[1, 1], v, kvc.at[1], end.at[1, 0], end.at[1, 1]]

    def q_of(row, start, size):
        return jnp.where(row == 0, q[pl.ds(start, size), :], qc[pl.ds(start, size), :])

    attend_kernel(frames, block, 2, index_ref, table_ref, q_of, ks, vs, o_ref)


def attend(index, table, j, frames, tokens, queries, k, v, kvc, kvp, end, partner):
    d = HEAD_DIM
    whole = pl.BlockSpec((2, ROWS, tokens, d), lambda r, ix, tb: (0, 0, 0, 0))
    own = pl.BlockSpec((tokens, d), lambda r, ix, tb: (0, ix[0] + j))
    crossed = pl.BlockSpec((2, tokens, d), lambda r, ix, tb: (0, 0, ix[1] + j))
    if partner:
        body = partner_kernel
        q_specs = [pl.BlockSpec((None, tokens, d), lambda r, ix, tb: (r, 0, 0))]
    else:
        body = own_kernel
        q_specs = [own, pl.BlockSpec((tokens, d), lambda r, ix, tb: (0, ix[1] + j))]
    return pl.pallas_call(
        functools.partial(body, frames, min(256, tokens)),
        out_shape=jax.ShapeDtypeStruct((ROWS, tokens, d), jnp.bfloat16),
        grid_spec=pltpu.PrefetchScalarGridSpec(
            num_scalar_prefetch=2,
            grid=(ROWS,),
            in_specs=q_specs + [whole, own, own, crossed, whole],
            out_specs=pl.BlockSpec((None, tokens, d), lambda r, ix, tb: (r, 0, 0)),
        ),
        compiler_params=pltpu.CompilerParams(vmem_limit_bytes=48 * 2**20),
        cost_estimate=pl.CostEstimate(
            flops=ROWS * 4 * tokens * 6 * tokens * d,
            transcendentals=ROWS * 6 * tokens * tokens,
            bytes_accessed=2 * tokens * d * (2 * ROWS * 6 + 8),
        ),
    )(index, table, *queries, kvp, k, v, kvc, end)


def project_kernel(pairs, parts, heads, index_ref, *refs):
    outs = heads
    o_refs = refs[:outs]
    w_refs = refs[outs : outs + 2 * pairs * parts]
    bias_ref, gate_ref, out_ref, attn, held, sems = refs[outs + 2 * pairs * parts :]
    step = pl.program_id(0)

    @pl.when(step == 0)
    def _():
        for i, w_ref in enumerate(w_refs):
            pltpu.make_async_copy(w_ref, held.at[i // parts, i % parts], sems.at[i]).start()
        for i, o_ref in enumerate(o_refs):
            at = pl.multiple_of(index_ref[2 * pairs + parts + i] * HEAD_DIM, HEAD_DIM)
            attn[:, pl.ds(at, HEAD_DIM)] = o_ref[...]

    for i in range(2 * pairs):

        @pl.when(step == i)
        def _():
            for p in range(parts):
                n = i * parts + p
                pltpu.make_async_copy(w_refs[n], held.at[i, p], sems.at[n]).wait()

    total = None
    rows = held.shape[2]
    for p in range(parts):
        at = pl.multiple_of(index_ref[2 * pairs + p] * rows, rows)
        d = jnp.dot(attn[:, pl.ds(at, rows)], held[step, p], preferred_element_type=jnp.float32)
        total = d if total is None else total + d
    out_ref[...] = ((total + bias_ref[...]) * gate_ref[...]).astype(out_ref.dtype)


def project(index, outs, blocks, out_bias, out_gate, pairs, parts):
    tokens = outs[0][0].shape[-2]
    rows, cols = blocks[0].shape
    heads = len(outs)
    width = heads * HEAD_DIM
    model = out_bias.shape[-1]
    o_specs = []
    for o, lead in outs:
        if lead:
            o_specs.append(pl.BlockSpec((None, tokens, HEAD_DIM), lambda s, ix: (0, 0, 0)))
        else:
            o_specs.append(pl.BlockSpec((tokens, HEAD_DIM), lambda s, ix: (0, 0)))
    by_step = pl.BlockSpec((1, cols), lambda s, ix: (0, ix[s]))
    return pl.pallas_call(
        functools.partial(project_kernel, pairs, parts, heads),
        out_shape=jax.ShapeDtypeStruct((tokens, model), jnp.bfloat16),
        grid_spec=pltpu.PrefetchScalarGridSpec(
            num_scalar_prefetch=1,
            grid=(2 * pairs,),
            in_specs=o_specs
            + [pl.BlockSpec(memory_space=pl.ANY)] * len(blocks)
            + [by_step, by_step],
            out_specs=pl.BlockSpec((tokens, cols), lambda s, ix: (0, ix[s])),
            scratch_shapes=[
                pltpu.VMEM((tokens, width), jnp.bfloat16),
                pltpu.VMEM((2 * pairs, parts, rows, cols), jnp.bfloat16),
                pltpu.SemaphoreType.DMA((len(blocks),)),
            ],
        ),
        compiler_params=pltpu.CompilerParams(vmem_limit_bytes=48 * 2**20),
        cost_estimate=pl.CostEstimate(
            flops=2 * tokens * width * model,
            transcendentals=0,
            bytes_accessed=2 * (width * model + tokens * model + tokens * width),
        ),
    )(index, *[o for o, _ in outs], *blocks, out_bias, out_gate)


def gather_weight(out_weight, w, group, parts, pairs, count):
    rows = out_weight.shape[0] // parts
    mine = lax.dynamic_slice_in_dim(out_weight, group * rows, rows, 0)
    theirs = lax.ppermute(mine, "wa", swaps(count))
    odd = (w % 2) == 1
    block = jnp.concatenate([jnp.where(odd, theirs, mine), jnp.where(odd, mine, theirs)], axis=1)
    turned = [block]
    for s in range(1, pairs):
        turned.append(lax.ppermute(block, "wa", [(i, (i + 2 * s) % count) for i in range(count)]))
    blocks = []
    for one in turned:
        for p in range(parts):
            if p == 0:
                blocks.append(one)
            else:
                perm = [(i, (i + p) % parts) for i in range(parts)]
                blocks.append(lax.ppermute(one, "groups", perm))
    return blocks + [lax.ppermute(b, "ha", [(0, 1), (1, 0)]) for b in blocks]


def on_device(queries, keys, values, tile_map, frame_offset, out_weight, out_bias, out_gate):
    frames, tile_h, tile_w, width = queries.shape
    tokens = frames * tile_h * tile_w
    count = lax.axis_size("wa")
    parts = lax.axis_size("groups")
    if lax.axis_size("ha") != ROWS or count % 2:
        raise ValueError("unsupported mesh")
    pairs = count // 2
    heads = width // HEAD_DIM
    core_heads = heads // 2
    each = core_heads // 2
    a = lax.axis_index("ha").astype(jnp.int32)
    w = lax.axis_index("wa").astype(jnp.int32)
    group = lax.axis_index("groups").astype(jnp.int32)
    y = w % 2
    cross = [(0, 1), (1, 0)]
    d = HEAD_DIM

    q = queries.reshape(tokens, width)
    k = keys.reshape(tokens, width)
    v = values.reshape(tokens, width)

    def cols(x, start, size):
        return lax.dynamic_slice_in_dim(x, start, size, x.ndim - 1)

    half = core_heads * d
    kvc = lax.ppermute(jnp.stack([cols(k, (1 - a) * half, half), cols(v, (1 - a) * half, half)]), "ha", cross)
    qc = lax.ppermute(cols(q, (1 - a) * half, half), "ha", cross)

    meta = jnp.concatenate([tile_map.reshape(1, 8), frame_offset.reshape(1, 1), jnp.zeros((1, 1), jnp.int32)], axis=1)
    meta = jnp.concatenate([meta, lax.ppermute(meta, "ha", cross)])
    meta = jnp.concatenate([lax.ppermute(meta, "wa", swaps(count)), meta])
    table = flag_table(meta, a, w, count)
    index = jnp.stack([a * core_heads + y * each, y * each])

    def both_rows(h):
        mine = jnp.stack([cols(k, (a * core_heads + h) * d, d), cols(v, (a * core_heads + h) * d, d)])
        return jnp.stack([mine, cols(kvc, h * d, d)], axis=1)

    kvp, qp, first, second = [], [], [], []
    for j in range(each):
        far = (1 - y) * each + j
        kvp.append(lax.ppermute(both_rows(far), "wa", swaps(count)))
        qs = jnp.stack([cols(q, (a * core_heads + far) * d, d), cols(qc, far * d, d)])
        qp.append(lax.ppermute(qs, "wa", swaps(count)))
        first.append(lax.ppermute(both_rows(y * each + j), "wa", outward(count)))
        second.append(lax.ppermute(kvp[j], "wa", inward(count)))

    wide = out_weight.shape[1] * 2
    aligned = wide % 128 == 0
    if aligned:
        blocks = gather_weight(out_weight, w, group, parts, pairs, count)
    own_o, part_o = [], []
    for j in range(each):
        o = attend(index, table, j, frames, tokens, [qp[j]], k, v, kvc, kvp[j], first[j], True)
        part_o.append(lax.ppermute(o, "wa", swaps(count)))
        own_o.append(attend(index, table, j, frames, tokens, [q, qc], k, v, kvc, kvp[j], second[j], False))

    outs, order = [], []
    for o, at in ((own_o, y * each), (part_o, (1 - y) * each)):
        for j in range(each):
            outs.append((o[j], True))
            order.append(a * core_heads + at + j)
            outs.append((lax.ppermute(o[j][1], "ha", cross), False))
            order.append((1 - a) * core_heads + at + j)

    if aligned:
        col = [c * pairs + (w // 2 - s) % pairs for c in (a, 1 - a) for s in range(pairs)]
        row = [(group - p) % parts for p in range(parts)]
        spots = jnp.stack(col + row + order)
        branch = project(spots, outs, blocks, out_bias[None], out_gate[None], pairs, parts)
    else:
        flat = jnp.zeros((tokens, width), jnp.bfloat16)
        for (o, lead), at in zip(outs, order):
            flat = lax.dynamic_update_slice_in_dim(flat, o[0] if lead else o, at * d, 1)
        weight = lax.all_gather(out_weight, ("ha", "wa"), axis=1, tiled=True)
        total = jnp.dot(flat, weight, preferred_element_type=jnp.float32)
        branch = ((total + out_bias) * out_gate).astype(jnp.bfloat16)
    return branch.reshape(frames, tile_h, tile_w, -1)


def solution(mesh):
    placed = (
        P("groups", "ha", "wa", None),
        P("groups", "ha", "wa", None),
        P("groups", "ha", "wa", None),
        P("ha", "wa", None),
        P("ha", "wa"),
        P(None, ("ha", "wa")),
        P(),
        P("groups"),
    )
    return jax.shard_map(
        on_device,
        mesh=mesh,
        in_specs=placed,
        out_specs=P("groups", "ha", "wa", None),
        check_vma=False,
    )
```

```python
import functools

import jax
import jax.numpy as jnp
from jax import lax
from jax.experimental import pallas as pl
from jax.experimental.pallas import tpu as pltpu
from jax.sharding import PartitionSpec as P


HEAD_DIM = 128
RADIUS = 2
LOG2E = 1.4426950408889634
NEG = -1e30
ROWS = 2
LATE = 4


def swaps(count):
    return [(i, i ^ 1) for i in range(count)]


def outward(count):
    return [(i, i - 2) for i in range(2, count, 2)] + [(i, i + 2) for i in range(1, count - 2, 2)]


def inward(count):
    return [(i, i + 2) for i in range(0, count - 2, 2)] + [(i, i - 2) for i in range(3, count, 2)]


def flag_table(meta, a, w, count):
    side = 1 - 2 * (w % 2)
    partner = w + side
    row = jnp.stack([a, 1 - a])
    q_col = jnp.stack([partner, partner, w, w])
    q_row = jnp.concatenate([row, row])
    k_col = jnp.stack([partner, w])
    ends = jnp.stack([partner + side, w - side])
    k_cols = jnp.concatenate(
        [
            jnp.broadcast_to(jnp.repeat(k_col, 2), (4, 4)),
            jnp.repeat(jnp.repeat(ends, 2)[:, None], 2, axis=1),
        ],
        axis=1,
    )
    k_rows = jnp.broadcast_to(jnp.tile(row, 3), (4, 6))
    d_row = k_rows - q_row[:, None]
    d_col = k_cols - q_col[:, None]
    spot = (d_row + 1) * 3 + d_col + 1
    own = spot == 4
    slot = spot - (spot > 4)
    hit = slot[:, :, None] == jnp.arange(8, dtype=jnp.int32)
    chosen = jnp.sum(jnp.where(hit, meta[:, None, :8], 0), axis=2) > 0
    inside = (k_cols >= 0) & (k_cols < count)
    flags = jnp.where(own, 2, (chosen & inside).astype(jnp.int32))
    return jnp.concatenate([flags, meta[:, 8:10]], axis=1).astype(jnp.int32)


def attend_kernel(frames, first, table_ref, q, k_refs, v_refs, o_ref):
    row = pl.program_id(0)
    tokens = o_ref.shape[0]
    area = tokens // frames
    scale = HEAD_DIM ** (-0.5) * LOG2E
    offset = table_ref[first + row, 6]
    q_frame = lax.broadcasted_iota(jnp.int32, (frames, tokens), 0)
    k_frame = lax.broadcasted_iota(jnp.int32, (frames, tokens), 1) // area
    near = jnp.where(jnp.abs(k_frame - q_frame - offset) <= RADIUS, 1, 0)

    def scores(t):
        flag = table_ref[first + row, t]
        bias = jnp.where((near * (flag & 1) + (flag >> 1)) > 0, 0.0, NEG).astype(jnp.float32)
        s = lax.dot_general(
            q, k_refs[t][...], (((1,), (1,)), ((), ())), preferred_element_type=jnp.float32
        )
        return (s.reshape(frames, area, tokens) + bias[:, None, :]).reshape(tokens, tokens)

    def lanes(x, op):
        return functools.reduce(op, [x[:, i : i + 128] for i in range(0, tokens, 128)])

    top = total = out = None
    coming = scores(0)
    for t in range(6):
        s = coming
        if t < 5:
            coming = scores(t + 1)
        peak = jnp.max(lanes(s, jnp.maximum), axis=-1, keepdims=True)
        if t > 0:
            peak = jnp.maximum(top, peak)
            keep = jnp.exp2((top - peak) * scale)
        p = jnp.exp2((s - peak) * scale)
        part = lanes(p, jnp.add)
        d = jnp.dot(p.astype(jnp.bfloat16), v_refs[t][...], preferred_element_type=jnp.float32)
        total = part if t == 0 else total * keep + part
        out = d if t == 0 else out * keep + d
        top = peak
    o_ref[...] = (out / jnp.sum(total, axis=-1, keepdims=True)).astype(o_ref.dtype)


def partner_kernel(frames, index_ref, table_ref, q, arrived, k, v, k_across, v_across, end, o_ref):
    ks = [arrived.at[0, 0], arrived.at[0, 1], k, k_across, end.at[0, 0], end.at[0, 1]]
    vs = [arrived.at[1, 0], arrived.at[1, 1], v, v_across, end.at[1, 0], end.at[1, 1]]
    attend_kernel(frames, 0, table_ref, q[...], ks, vs, o_ref)


def own_kernel(frames, index_ref, table_ref, q, q_across, arrived, k, v, k_across, v_across, end, o_ref):
    ks = [arrived.at[0, 0], arrived.at[0, 1], k, k_across, end.at[0, 0], end.at[0, 1]]
    vs = [arrived.at[1, 0], arrived.at[1, 1], v, v_across, end.at[1, 0], end.at[1, 1]]
    chosen = jnp.where(pl.program_id(0) == 0, q[...], q_across[...])
    attend_kernel(frames, 2, table_ref, chosen, ks, vs, o_ref)


def attend(index, table, j, q_spot, e_spot, frames, tokens, queries, kv, across, arrived, end):
    d = HEAD_DIM
    own = pl.BlockSpec((tokens, d), lambda r, ix, tb: (0, ix[0] + j))
    whole = pl.BlockSpec((2, ROWS, tokens, d), lambda r, ix, tb: (0, 0, 0, 0))
    last = pl.BlockSpec((2, ROWS, tokens, d), lambda r, ix, tb: (0, 0, 0, e_spot))
    if len(queries) == 2:
        body, q_specs = own_kernel, [own, own]
    else:
        body, q_specs = partner_kernel, [pl.BlockSpec((None, tokens, d), lambda r, ix, tb: (r, 0, q_spot))]
    return pl.pallas_call(
        functools.partial(body, frames),
        out_shape=jax.ShapeDtypeStruct((ROWS, tokens, d), jnp.bfloat16),
        grid_spec=pltpu.PrefetchScalarGridSpec(
            num_scalar_prefetch=2,
            grid=(ROWS,),
            in_specs=q_specs + [whole, own, own, own, own, last],
            out_specs=pl.BlockSpec((None, tokens, d), lambda r, ix, tb: (r, 0, 0)),
        ),
        compiler_params=pltpu.CompilerParams(vmem_limit_bytes=48 * 2**20),
        cost_estimate=pl.CostEstimate(
            flops=ROWS * 4 * tokens * 6 * tokens * d,
            transcendentals=ROWS * 6 * tokens * tokens,
            bytes_accessed=2 * tokens * d * (2 * ROWS * 6 + 8),
        ),
    )(index, table, *queries, arrived, *kv, *across, end)


def early_kernel(pairs, parts, heads, aligned, index_ref, *refs):
    blocks = 2 * pairs * parts
    o_refs = refs[:heads]
    w_refs = refs[heads : heads + blocks]
    out_ref, rest_ref, attn, held, sems = refs[heads + blocks :]
    step = pl.program_id(0)
    steps = held.shape[0] // out_ref.shape[1]
    size = w_refs[0].shape[1]
    cols = held.shape[0] // steps
    base = steps + 2 * blocks

    def copies(i):
        found = []
        for n in range(i * parts, (i + 1) * parts):
            for h in range(2):
                at = pl.multiple_of(index_ref[steps + 2 * n + h] * size, size)
                found.append(pltpu.make_async_copy(w_refs[n].at[h], held.at[pl.ds(at, size)], sems.at[n, h]))
        return found

    @pl.when(step == 0)
    def _():
        for i in range(2 * pairs):
            for copy in copies(i):
                copy.start()
        for i, o_ref in enumerate(o_refs):
            at = pl.multiple_of(index_ref[base + i] * HEAD_DIM, HEAD_DIM)
            attn[:, pl.ds(at, HEAD_DIM)] = o_ref[...]
        for i in range(LATE):
            at = pl.multiple_of(index_ref[base + heads + i] * HEAD_DIM, HEAD_DIM)
            attn[:, pl.ds(at, HEAD_DIM)] = jnp.zeros((attn.shape[0], HEAD_DIM), attn.dtype)

    for i in range(2 * pairs):

        @pl.when(step == (i if aligned else 0))
        def _():
            for copy in copies(i):
                copy.wait()

    at = pl.multiple_of(index_ref[step] * cols, cols)
    for i in range(LATE):
        lane = pl.multiple_of(index_ref[base + heads + i] * HEAD_DIM, HEAD_DIM)
        rest_ref[:, i * HEAD_DIM : (i + 1) * HEAD_DIM] = held[pl.ds(at, cols), pl.ds(lane, HEAD_DIM)]
    out_ref[...] = lax.dot_general(
        attn[...], held[pl.ds(at, cols), :], (((1,), (1,)), ((), ())), preferred_element_type=jnp.float32
    )


def late_kernel(partial, rest, *refs):
    bias, gate, out = refs[LATE:]
    attn = jnp.concatenate([ref[...] for ref in refs[:LATE]], axis=1)
    total = partial[...] + lax.dot_general(
        attn, rest[...], (((1,), (1,)), ((), ())), preferred_element_type=jnp.float32
    )
    out[...] = ((total + bias[...]) * gate[...]).astype(out.dtype)


def project(index, outs, blocks, out_bias, out_gate, pairs, parts, aligned):
    tokens = outs[0][0].shape[-2]
    _, width = blocks[0].shape[1:]
    heads = len(outs) - LATE
    model = out_bias.shape[-1]
    cols = model // (2 * pairs) if aligned else 128
    row_of = {row: pl.BlockSpec((None, tokens, HEAD_DIM), lambda s, *ix, row=row: (row, 0, 0)) for row in (0, 1)}
    o_specs = [row_of[row] for _, row in outs]
    arrays = [o for o, _ in outs]
    steps = model // cols
    partial, rest = pl.pallas_call(
        functools.partial(early_kernel, pairs, parts, heads, aligned),
        out_shape=(
            jax.ShapeDtypeStruct((tokens, model), jnp.float32),
            jax.ShapeDtypeStruct((model, LATE * HEAD_DIM), jnp.bfloat16),
        ),
        grid_spec=pltpu.PrefetchScalarGridSpec(
            num_scalar_prefetch=1,
            grid=(steps,),
            in_specs=o_specs[:heads] + [pl.BlockSpec(memory_space=pltpu.MemorySpace.HBM)] * len(blocks),
            out_specs=(
                pl.BlockSpec((tokens, cols), lambda s, ix: (0, ix[s])),
                pl.BlockSpec((cols, LATE * HEAD_DIM), lambda s, ix: (ix[s], 0)),
            ),
            scratch_shapes=[
                pltpu.VMEM((tokens, width), jnp.bfloat16),
                pltpu.VMEM((model, width), jnp.bfloat16),
                pltpu.SemaphoreType.DMA((len(blocks), 2)),
            ],
        ),
        compiler_params=pltpu.CompilerParams(vmem_limit_bytes=40 * 2**20),
        cost_estimate=pl.CostEstimate(
            flops=2 * tokens * width * model,
            transcendentals=0,
            bytes_accessed=2 * (width * model + 2 * tokens * model + tokens * width),
        ),
    )(index, *arrays[:heads], *blocks)
    by_step = pl.BlockSpec((1, cols), lambda s: (0, s))
    return pl.pallas_call(
        late_kernel,
        out_shape=jax.ShapeDtypeStruct((tokens, model), jnp.bfloat16),
        grid_spec=pl.GridSpec(
            grid=(steps,),
            in_specs=[
                pl.BlockSpec((tokens, cols), lambda s: (0, s)),
                pl.BlockSpec((cols, LATE * HEAD_DIM), lambda s: (s, 0)),
                *o_specs[heads:],
                by_step,
                by_step,
            ],
            out_specs=pl.BlockSpec((tokens, cols), lambda s: (0, s)),
        ),
        compiler_params=pltpu.CompilerParams(vmem_limit_bytes=32 * 2**20),
        cost_estimate=pl.CostEstimate(
            flops=2 * LATE * tokens * HEAD_DIM * model,
            transcendentals=0,
            bytes_accessed=6 * tokens * model,
        ),
    )(partial, rest, *arrays[heads:], out_bias, out_gate)


def on_device(queries, keys, values, tile_map, frame_offset, out_weight, out_bias, out_gate):
    frames, tile_h, tile_w, width = queries.shape
    tokens = frames * tile_h * tile_w
    count = lax.axis_size("wa")
    parts = lax.axis_size("groups")
    if lax.axis_size("ha") != ROWS or count % 2:
        raise ValueError("unsupported mesh")
    pairs = count // 2
    heads = width // HEAD_DIM
    core_heads = heads // 2
    each = core_heads // 2
    a = lax.axis_index("ha").astype(jnp.int32)
    w = lax.axis_index("wa").astype(jnp.int32)
    group = lax.axis_index("groups").astype(jnp.int32)
    y = w % 2
    cross = [(0, 1), (1, 0)]
    d = HEAD_DIM

    q = queries.reshape(tokens, width)
    k = keys.reshape(tokens, width)
    v = values.reshape(tokens, width)

    def cols(x, start, size):
        return lax.dynamic_slice_in_dim(x, start, size, x.ndim - 1)

    def turn(s):
        return [(i, (i + 2 * s) % count) for i in range(count)]

    shard = out_weight.T
    size = shard.shape[0] // parts
    small = jnp.concatenate([tile_map.reshape(1, 8), frame_offset.reshape(1, 1)], axis=1).astype(jnp.bfloat16)
    piece = lax.dynamic_slice_in_dim(shard, group * size, size, 0)
    mine = jnp.concatenate([piece, jnp.pad(small, ((0, 7), (0, width - 9)))])
    theirs = lax.ppermute(mine, "wa", swaps(count))

    k_across = lax.ppermute(k, "ha", cross)
    v_across = lax.ppermute(v, "ha", cross)
    q_across = lax.ppermute(q, "ha", cross)
    index = jnp.stack([a * core_heads + y * each])

    def pack_kv(h, n):
        at = (a * core_heads + h) * d
        ks = jnp.stack([cols(k, at, n * d), cols(k_across, at, n * d)])
        vs = jnp.stack([cols(v, at, n * d), cols(v_across, at, n * d)])
        return jnp.stack([ks, vs])

    def pack_q(h, n):
        at = (a * core_heads + h) * d
        return jnp.stack([cols(q, at, n * d), cols(q_across, at, n * d)])

    far = (1 - y) * each
    out_kv = [pack_kv(far + j, 1) for j in range(each)]
    out_z = [pack_kv(y * each + j, 1) for j in range(each)]
    theirs, out_z[1] = lax.optimization_barrier((theirs, out_z[1]))
    arrived = [lax.ppermute(out_kv[j], "wa", swaps(count)) for j in range(each)]
    first = [lax.ppermute(out_z[j], "wa", outward(count)) for j in range(each)]
    second = [lax.ppermute(arrived[j], "wa", inward(count)) for j in range(each)]
    asked = [
        lax.ppermute(pack_q(far, 1), "wa", swaps(count)), lax.ppermute(pack_q(far + 1, each - 1), "wa", swaps(count))
    ]

    block = jnp.stack([piece, theirs[:size]])
    meta = jnp.stack([theirs[size, :16], mine[size, :16]]).astype(jnp.int32)
    other = lax.ppermute(meta, "ha", cross)
    meta = jnp.stack([meta[0], other[0], meta[1], other[1]])
    table = flag_table(meta, a, w, count)

    turned = [block]
    for _ in range(1, pairs):
        turned.append(lax.ppermute(turned[-1], "wa", turn(1)))
    blocks = []
    for s in range(pairs):
        for p in range(parts):
            perm = [(i, (i + p) % parts) for i in range(parts)]
            blocks.append(turned[s] if p == 0 else lax.ppermute(turned[s], "groups", perm))
    blocks += [lax.ppermute(b, "ha", cross) for b in blocks]

    outs = []
    kv, over = (k, v), (k_across, v_across)
    for j in range(each):
        queries, spot = (asked[0], 0) if j == 0 else (asked[1], j - 1)
        o = attend(index, table, j, spot, 0, frames, tokens, [queries], kv, over, arrived[j], first[j])
        back = lax.ppermute(o, "wa", swaps(count))
        o = attend(index, table, j, 0, 0, frames, tokens, [q, q_across], kv, over, arrived[j], second[j])
        for o, at in ((o, y * each + j), (back, far + j)):
            outs.append((o, 0, a * core_heads + at))
            outs.append((lax.ppermute(o, "ha", cross), 1, (1 - a) * core_heads + at))
    order = [at for _, _, at in outs]
    outs = [(o, row) for o, row, _ in outs]

    aligned = (2 * shard.shape[0]) % 128 == 0
    chunks, pieces = [], []
    for c in (a, 1 - a):
        for s in range(pairs):
            pair = (w // 2 - s) % pairs
            chunks.append(c * pairs + pair)
            for p in range(parts):
                for h in range(2):
                    column = c * count + 2 * pair + (y + h) % 2
                    pieces.append(column * parts + (group - p) % parts)
    if not aligned:
        chunks = [jnp.int32(i) for i in range(out_bias.shape[0] // 128)]
    branch = project(jnp.stack(chunks + pieces + order), outs, blocks, out_bias[None], out_gate[None], pairs, parts, aligned)
    return branch.reshape(frames, tile_h, tile_w, -1)


def solution(mesh):
    placed = (
        P("groups", "ha", "wa", None),
        P("groups", "ha", "wa", None),
        P("groups", "ha", "wa", None),
        P("ha", "wa", None),
        P("ha", "wa"),
        P(None, ("ha", "wa")),
        P(),
        P("groups"),
    )

    return jax.shard_map(
        on_device,
        mesh=mesh,
        in_specs=placed,
        out_specs=P("groups", "ha", "wa", None),
        check_vma=False,
    )
```
